128 devices in a mesh: fsdp: 8 (over y_lo, z), seq: 16 (over x, y_hi, core).
Axes of the slice: x: 4, y: 4 (y_hi: 2, y_lo: 2; y = y_hi * 2 + y_lo), z: 4, core: 2. Of those that a mesh axis runs over, the one named last changes fastest.
Arguments:
- tokens: bfloat16 [7168, 4096], P(('fsdp', 'seq')), may hold values from -6 to 6
- grad_out: bfloat16 [7168, 4096], P(('fsdp', 'seq')), may hold values from -6 to 6
- gate_weight: bfloat16 [4096, 14336], P('fsdp', 'seq'), may hold values from -0.09375 to 0.09375
- up_weight: bfloat16 [4096, 14336], P('fsdp', 'seq'), may hold values from -0.09375 to 0.09375
- down_weight: bfloat16 [14336, 4096], P('seq', 'fsdp'), may hold values from -0.09375 to 0.09375
- keep_mask: int32 [8, 112], P(None, 'seq'), may hold values from 0 to 1, as said below
- task_ids: int32 [7168], P('fsdp'), may hold values from 0 to 7
Outputs:
- layer_out: bfloat16 [7168, 4096], P(('fsdp', 'seq'))
- input_grad: bfloat16 [7168, 4096], P(('fsdp', 'seq'))
The draws below stay inside these ranges and needn't reach their ends.
Inputs may be any that keep to these rules, and one draw needn't show every extreme that they name: `keep_mask`: entries are 0 or 1. In each aligned group of 7 consecutive blocks at most 4 blocks are kept by some task, and exactly 4 in at least one group; the other blocks of a group are kept by no task.
All inputs are finite; a program needn't handle non-finite values.
Results may differ from the reference program's by a relative error of at most 0.014.
Values may be sent and summed in bfloat16 or wider, within the bound.
A program may use at most 128 MiB of HBM per device.

```python
import jax
import jax.numpy as jnp
from jax import lax

D = 4096
FF = 14336
BLOCK = 128
NTASK = 8
TOKENS = 7168
NB = 112
NB_LOC = 7
LIVE_LOC = 4
N_SEQ = 16


def draw_keep_mask(key, part):
    groups = NB // NB_LOC
    keys = jax.random.split(key, 6)
    counts = jax.random.randint(keys[0], (groups,), (LIVE_LOC + 1) // 2, LIVE_LOC + 1)
    full_group = jax.random.randint(keys[1], (), 0, groups)
    counts = jnp.where(jnp.arange(groups, dtype=jnp.int32) == full_group, LIVE_LOC, counts)
    shuffled = jax.vmap(lambda single: jax.random.permutation(single, NB_LOC))(jax.random.split(keys[2], groups))
    positions = jnp.argsort(shuffled, axis=1)
    live_blocks = (positions < counts[:, None]).reshape(NB)
    thresholds = jax.random.randint(keys[3], (NTASK, 1), 1, 10)
    dice_rolls = jax.random.randint(keys[4], (NTASK, NB), 0, 10)
    kept_blocks = dice_rolls < thresholds
    owner_task = jax.random.randint(keys[5], (NB,), 0, NTASK)
    kept_blocks = kept_blocks | (jnp.arange(NTASK, dtype=jnp.int32)[:, None] == owner_task[None, :])
    return (kept_blocks & live_blocks[None, :]).astype(jnp.int32)


def set_ends(entries, key, low, high):
    shape = entries.shape
    index_at = [jax.random.randint(jax.random.fold_in(key, axis), (), 0, shape[axis]) for axis in range(len(shape))]
    entries = entries.at[tuple(index_at)].set(low)
    longest = shape.index(max(shape))
    index_at[longest] = (index_at[longest] + 1) % shape[longest]
    return entries.at[tuple(index_at)].set(high)


def levels(key, dims, shards, low, high):
    def one(position, parts):
        heights = jax.random.uniform(jax.random.fold_in(jax.random.fold_in(key, 6), position), (parts,), jnp.float32, low / len(shards), high / len(shards))
        return jnp.repeat(jnp.exp(heights), dims[position] // parts).reshape((-1,) + (1,) * (len(dims) - position - 1))

    gain = one(*shards[0])
    for cut in shards[1:]:
        gain = gain * one(*cut)
    return gain


def normal_values(own_key, shape, width, limit, shards=(), kind=jnp.bfloat16):
    values = width * jax.random.normal(own_key, shape, jnp.float32)
    if shards:
        values = values * levels(own_key, shape, shards, -0.22, 0.18)
    return jnp.clip(values, -limit, limit).astype(kind)


def setup_inputs(seed: int = 0) -> dict:
    arg_keys = jax.random.split(jax.random.key(seed), 8)
    tokens = normal_values(arg_keys[0], (TOKENS, D), 1.0, 6.0, ((0, 128),))
    grad_out = normal_values(arg_keys[1], (TOKENS, D), 1.0, 6.0, ((0, 128),))
    gate_weight = normal_values(arg_keys[2], (D, FF), D ** -0.5, 0.09375, ((0, 8), (1, 16)))
    up_weight = normal_values(arg_keys[3], (D, FF), D ** -0.5, 0.09375, ((0, 8), (1, 16)))
    down_weight = normal_values(arg_keys[4], (FF, D), (FF // 4) ** -0.5, 0.09375, ((0, 16), (1, 8)))
    keep_mask = draw_keep_mask(jax.random.fold_in(arg_keys[7], 71), 0)
    task_ids = set_ends(jax.random.randint(arg_keys[6], (TOKENS,), 0, NTASK), jax.random.fold_in(arg_keys[6], 1), 0, NTASK - 1).astype(jnp.int32)
    return {"tokens": tokens, "grad_out": grad_out, "gate_weight": gate_weight, "up_weight": up_weight, "down_weight": down_weight, "keep_mask": keep_mask, "task_ids": task_ids}


def transposed(left, right):
    return lax.dot_general(left, right, (((1,), (1,)), ((), ())), preferred_element_type=jnp.float32)


def reference(tokens, grad_out, gate_weight, up_weight, down_weight, keep_mask, task_ids):
    onehot_tasks = (task_ids[:, None] == jnp.arange(NTASK, dtype=jnp.int32)[None, :]).astype(jnp.float32)
    row_keep = jnp.dot(onehot_tasks, keep_mask.astype(jnp.float32))
    neuron_mask = jnp.repeat(row_keep, BLOCK, axis=1)
    gate_pre = jnp.dot(tokens, gate_weight, preferred_element_type=jnp.float32)
    up_pre = jnp.dot(tokens, up_weight, preferred_element_type=jnp.float32)
    logistic = jax.nn.sigmoid(gate_pre)
    activated = gate_pre * logistic
    hidden = (activated * up_pre * neuron_mask).astype(jnp.bfloat16)
    hidden_grad = transposed(grad_out, down_weight)
    masked_grad = hidden_grad * neuron_mask
    gate_grad = (masked_grad * up_pre * logistic * (1.0 + gate_pre * (1.0 - logistic))).astype(jnp.bfloat16)
    up_grad = (masked_grad * activated).astype(jnp.bfloat16)
    group_width = FF // N_SEQ

    def add_group(totals, group):
        start = (group * group_width).astype(jnp.int32)
        hidden_piece = lax.dynamic_slice_in_dim(hidden, start, group_width, 1)
        down_piece = lax.dynamic_slice_in_dim(down_weight, start, group_width, 0)
        gate_piece = lax.dynamic_slice_in_dim(gate_grad, start, group_width, 1)
        up_piece = lax.dynamic_slice_in_dim(up_grad, start, group_width, 1)
        gate_cols = lax.dynamic_slice_in_dim(gate_weight, start, group_width, 1)
        up_cols = lax.dynamic_slice_in_dim(up_weight, start, group_width, 1)
        out_part = jnp.dot(hidden_piece, down_piece, preferred_element_type=jnp.float32).astype(jnp.bfloat16)
        grad_part = (transposed(gate_piece, gate_cols) + transposed(up_piece, up_cols)).astype(jnp.bfloat16)
        out_part, grad_part = lax.optimization_barrier((out_part, grad_part))
        return (totals[0] + out_part.astype(jnp.float32), totals[1] + grad_part.astype(jnp.float32)), None

    empty = jnp.zeros((tokens.shape[0], D), jnp.float32)
    sums, unused = lax.scan(add_group, (empty, empty), jnp.arange(N_SEQ, dtype=jnp.int32))
    return sums[0].astype(jnp.bfloat16), sums[1].astype(jnp.bfloat16)
```

```python
import functools

import jax
import jax.numpy as jnp
from jax import lax
from jax.experimental import pallas as pl
from jax.experimental.pallas import tpu as pltpu
from jax.sharding import PartitionSpec as P

MESH = pl.DeviceIdType.MESH
F32, BF16 = jnp.float32, jnp.bfloat16
RING, PAIRS, SLOTS = 4, 4, 8
KEPT, BLOCK, TASKS = 4, 128, 8
TOK, GRAD, GATE, UP, DOWN = range(5)
BY_PAIR = (GATE, UP, DOWN)


def dot(left, right):
    return jnp.dot(left, right, preferred_element_type=F32)


def dot_t(left, right):
    return lax.dot_general(left, right, (((1,), (1,)), ((), ())), preferred_element_type=F32)


def kernel(
    keep_ref, tok_ref, grad_ref, gate_ref, up_ref, down_ref, onehot_ref, out_ref, ig_ref,
    rows_buf, w_buf, cols_stage, rows_stage, keep_buf, acc, hid, gate_g, up_g, part, inbox,
    local_sem, send_sem, recv_sem, core_send, core_recv, rs_send, rs_recv,
):
    f, s = lax.axis_index("fsdp"), lax.axis_index("seq")
    z, yl = f % RING, f // RING
    x, yh, core = s // 4, (s // 2) % 2, s % 2
    x_up = {"seq": ((x + 1) % RING) * 4 + yh * 2 + core}
    x_down = {"seq": ((x + RING - 1) % RING) * 4 + yh * 2 + core}
    y_far = {"seq": x * 4 + (1 - yh) * 2 + core}
    sibling = {"seq": x * 4 + yh * 2 + 1 - core}
    z_up = {"fsdp": yl * RING + (z + 1) % RING}
    z_down = {"fsdp": yl * RING + (z + RING - 1) % RING}
    y_near = {"fsdp": (1 - yl) * RING + z}

    width = w_buf.shape[-1]
    chunk = tok_ref.shape[0]
    n_rows = SLOTS * chunk

    def owner(k):
        offset = (0, 0, 1, RING - 1, 1, RING - 1, 2, 2)[k]
        other = k in (1, 4, 5, 7)
        return ((1 - yl) if other else yl) * RING + (z + offset) % RING

    def columns(k):
        return pl.ds(pl.multiple_of(owner(k) * width, width), width)

    def slot(array, k):
        if array in (TOK, GRAD):
            return rows_buf.at[array, k]
        return w_buf.at[array - GATE, 0, k]

    def neighbours(array):
        return (x_up, x_down, y_far) if array in (TOK, GRAD) else (z_up, z_down, y_near)

    sent = []

    def send(src, dst, ssem, rsem, device):
        copy = pltpu.make_async_remote_copy(
            src_ref=src, dst_ref=dst, send_sem=ssem, recv_sem=rsem, device_id=device,
            device_id_type=MESH,
        )
        copy.start()
        sent.append(copy)

    def arrived(dst, rsem, device):
        pltpu.make_async_remote_copy(
            src_ref=dst, dst_ref=dst, send_sem=local_sem.at[0], recv_sem=rsem, device_id=device,
            device_id_type=MESH,
        ).wait_recv()

    half = width // 2

    def part_of(ref, which):
        return ref if which is None else ref.at[pl.ds(which * half, half)]

    def spread(array, k, lane, to, which=None, src=None, hop=None):
        source = slot(array, k) if src is None else src
        send(
            part_of(source, which), part_of(slot(array, to), which), send_sem.at[array, lane],
            recv_sem.at[array, to if which in (None, 0) else SLOTS + to - 6], neighbours(array)[hop],
        )

    def got(array, k, which=None):
        hop = (None, 2, 0, 1, 0, 1, 1, 1)[k]
        if which is not None:
            hop = (1, 0)[which] if k == 6 else 2
        sem = recv_sem.at[array, k if which in (None, 0) else SLOTS + k - 6]
        arrived(part_of(slot(array, k), which), sem, neighbours(array)[hop])

    def to_sibling(array, k):
        w = array - GATE
        send(w_buf.at[w, 0, k], w_buf.at[w, 1, k], core_send.at[w, k], core_recv.at[w, k], sibling)

    def from_sibling(array, k):
        w = array - GATE
        arrived(w_buf.at[w, 1, k], core_recv.at[w, k], sibling)

    def first(array, src=None):
        spread(array, 0, 0, 1, src=src, hop=2)
        spread(array, 0, 1, 3, src=src, hop=0)
        spread(array, 0, 2, 2, src=src, hop=1)
        if array >= GATE:
            to_sibling(array, 0)

    def second(array):
        got(array, 1)
        spread(array, 1, 3, 5, hop=0)
        spread(array, 1, 4, 4, hop=1)
        if array >= GATE:
            to_sibling(array, 1)

    def third(array):
        got(array, 3)
        if array in BY_PAIR:
            spread(array, 3, 5, 6, which=0, hop=0)
        else:
            spread(array, 3, 5, 6, hop=0)
        if array >= GATE:
            to_sibling(array, 3)
        got(array, 2)
        if array in BY_PAIR:
            spread(array, 2, 6, 6, which=1, hop=1)
        if array >= GATE:
            to_sibling(array, 2)

    def fourth(array):
        got(array, 4)
        if array not in BY_PAIR:
            spread(array, 4, 6, 7, hop=1)
        got(array, 5)
        if array >= GATE:
            to_sibling(array, 4)
            to_sibling(array, 5)

    def fifth(array):
        if array in BY_PAIR:
            got(array, 6, 0)
            spread(array, 6, 7, 7, which=0, hop=2)
            got(array, 6, 1)
            spread(array, 6, 8, 7, which=1, hop=2)
        else:
            got(array, 6)
        if array >= GATE:
            to_sibling(array, 6)

    def sixth(array):
        if array in BY_PAIR:
            got(array, 7, 0)
            got(array, 7, 1)
        else:
            hop = neighbours(array)[0]
            arrived(slot(array, 7), recv_sem.at[array, 7], hop)
        if array >= GATE:
            to_sibling(array, 7)

    barrier = pltpu.get_barrier_semaphore()
    around = (x_up, x_down, y_far, sibling, z_up, z_down, y_near)
    for device in around:
        pl.semaphore_signal(barrier, inc=1, device_id=device, device_id_type=MESH)
    stage = (
        pltpu.make_async_copy(gate_ref, cols_stage.at[0], local_sem.at[1]),
        pltpu.make_async_copy(up_ref, cols_stage.at[1], local_sem.at[2]),
        pltpu.make_async_copy(down_ref, rows_stage, local_sem.at[3]),
        pltpu.make_async_copy(tok_ref, rows_buf.at[TOK, 0], local_sem.at[4]),
        pltpu.make_async_copy(grad_ref, rows_buf.at[GRAD, 0], local_sem.at[5]),
    )
    for copy in stage:
        copy.start()

    n_blocks = keep_ref.shape[1]
    spare = n_blocks - KEPT
    alive = []
    for b in range(n_blocks):
        seen = keep_ref[0, b]
        for t in range(1, TASKS):
            seen = jnp.maximum(seen, keep_ref[t, b])
        alive.append(seen)
    room = KEPT - sum(alive[1:], alive[0])
    taken, place, before = [], [], jnp.int32(0)
    for b in range(n_blocks):
        fill = (1 - alive[b]) * jnp.where(room > 0, 1, 0)
        room = room - fill
        taken.append(alive[b] + fill)
        place.append(before)
        before = before + taken[b]
    picks = [
        [(b, taken[b] * jnp.where(place[b] == j, 1, 0)) for b in range(j, j + spare + 1)]
        for j in range(KEPT)
    ]

    pl.semaphore_wait(barrier, len(around))
    first(TOK, tok_ref)

    def blend(terms, shape):
        blend_of = None
        for take, block in terms:
            term = block * jnp.full(shape, take.astype(F32)).astype(BF16)
            blend_of = term if blend_of is None else blend_of + term
        return blend_of

    def pack_columns(array):
        w = array - GATE
        stage[w].wait()
        step = 64

        @pl.loop(0, w_buf.shape[3] // step)
        def _(i):
            at = pl.ds(pl.multiple_of(i * step, step), step)
            for j in range(KEPT):
                terms = [(take, cols_stage[w, at, b * BLOCK : (b + 1) * BLOCK]) for b, take in picks[j]]
                w_buf[w, 0, 0, at, j * BLOCK : (j + 1) * BLOCK] = blend(terms, (step, BLOCK))

    pack_columns(GATE)
    pack_columns(UP)
    stage[2].wait()
    step = 32

    @pl.loop(0, BLOCK // step)
    def _(i):
        for j in range(KEPT):
            terms = [
                (take, rows_stage[pl.ds(pl.multiple_of(b * BLOCK + i * step, step), step), :])
                for b, take in picks[j]
            ]
            at = pl.ds(pl.multiple_of(j * BLOCK + i * step, step), step)
            w_buf[2, 0, 0, at, :] = blend(terms, (step, width))

    task_row = lax.broadcasted_iota(jnp.int32, (keep_buf.shape[1], BLOCK), 0)
    for j in range(KEPT):
        block = jnp.zeros((keep_buf.shape[1], BLOCK), F32)
        for t in range(TASKS):
            kept = sum(take * keep_ref[t, b] for b, take in picks[j])
            block = jnp.where(task_row == t, kept.astype(F32), block)
        keep_buf[0, :, j * BLOCK : (j + 1) * BLOCK] = block.astype(BF16)

    first(GATE)
    first(UP)
    first(GRAD, grad_ref)
    send(keep_buf.at[0], keep_buf.at[1], core_send.at[3, 0], core_recv.at[3, 0], sibling)
    stage[3].wait()
    stage[4].wait()

    second(TOK)
    second(GATE)
    third(GATE)
    second(UP)
    third(TOK)
    third(UP)
    second(GRAD)
    first(DOWN)
    fourth(TOK)
    fourth(GATE)
    third(GRAD)
    fifth(TOK)
    sixth(TOK)

    def rows(array, k):
        return rows_buf[array, :, :, columns(k)].reshape(n_rows, width)

    def group(c):
        return pl.ds(pl.multiple_of(c * width, width), width)

    def forward(j):
        a, b = 2 * j, 2 * j + 1
        for array in (GATE, UP):
            from_sibling(array, a)
            from_sibling(array, b)

        @pl.loop(0, 2)
        def _(c):
            for w in range(2):
                new = dot(rows(TOK, a), w_buf[w, c, a]) + dot(rows(TOK, b), w_buf[w, c, b])
                if j:
                    new = acc[w, :, group(c)] + new
                acc[w, :, group(c)] = new

    def backward(j):
        a, b = 2 * j, 2 * j + 1

        @pl.loop(0, 2)
        def _(c):
            new = dot_t(rows(GRAD, a), w_buf[2, c, a]) + dot_t(rows(GRAD, b), w_buf[2, c, b])
            if j:
                new = acc[2, :, group(c)] + new
            acc[2, :, group(c)] = new

    def activate():
        step = 32

        @pl.loop(0, n_rows // step)
        def _(i):
            at = pl.ds(pl.multiple_of(i * step, step), step)
            for c in range(2):
                cols = slice(c * width, (c + 1) * width)
                mask = dot(onehot_ref[at, :], keep_buf[c])
                gate_pre, up_pre = acc[0, at, cols], acc[1, at, cols]
                logistic = jax.nn.sigmoid(gate_pre)
                activated = gate_pre * logistic * mask
                hid[at, cols] = (activated * up_pre).astype(BF16)
                acc[0, at, cols] = mask * up_pre * logistic * (1.0 + gate_pre * (1.0 - logistic))
                acc[1, at, cols] = activated

    def pull_back():
        step = 32

        @pl.loop(0, n_rows // step)
        def _(i):
            at = pl.ds(pl.multiple_of(i * step, step), step)
            hidden_grad = acc[2, at, :]
            gate_g[at, :] = (hidden_grad * acc[0, at, :]).astype(BF16)
            up_g[at, :] = (hidden_grad * acc[1, at, :]).astype(BF16)

    def out_part(j):
        @pl.loop(2 * j, 2 * j + 2)
        def _(k):
            new = dot(hid[:, :width], w_buf[2, 0, k]) + dot(hid[:, width:], w_buf[2, 1, k])
            part[0, k] = new.reshape(SLOTS, chunk, width).astype(BF16)

    def grad_part(j):
        @pl.loop(2 * j, 2 * j + 2)
        def _(k):
            new = dot_t(gate_g[:, :width], w_buf[0, 0, k]) + dot_t(gate_g[:, width:], w_buf[0, 1, k])
            new += dot_t(up_g[:, :width], w_buf[1, 0, k]) + dot_t(up_g[:, width:], w_buf[1, 1, k])
            part[1, k] = new.reshape(SLOTS, chunk, width).astype(BF16)

    def piece(o, j, at):
        return part.at[o, pl.ds(2 * j, 2), at]

    def post(o, j, at, m, device):
        send(piece(o, j, at), inbox.at[o, j, m], rs_send.at[o, j, m], rs_recv.at[o, j, m], device)

    def collect(o, j, m):
        device = (x_down, x_up, x_down, x_up, x_down, x_up, y_far)[m]
        arrived(inbox.at[o, j, m], rs_recv.at[o, j, m], device)

    def sum_a(o, j):
        post(o, j, 6, 0, x_up)
        post(o, j, 7, 1, x_down)
        post(o, j, 4, 2, x_up)
        post(o, j, 3, 3, x_down)

    def sum_b(o, j):
        for m, at, device in ((0, 2, x_up), (1, 5, x_down)):
            collect(o, j, m)
            for i in range(2):
                both = part[o, 2 * j + i, at].astype(F32) + inbox[o, j, m, i].astype(F32)
                part[o, 2 * j + i, at] = both.astype(BF16)
            post(o, j, at, 4 + m, device)

    def sum_c(o, j):
        for m in (2, 3, 4, 5):
            collect(o, j, m)
        for i in range(2):
            both = part[o, 2 * j + i, 1].astype(F32) + inbox[o, j, 2, i].astype(F32)
            part[o, 2 * j + i, 1] = (both + inbox[o, j, 5, i].astype(F32)).astype(BF16)
        post(o, j, 1, 6, y_far)

    def sum_d(o, j):
        collect(o, j, 6)
        result = out_ref if o == 0 else ig_ref
        for i in range(2):
            both = part[o, 2 * j + i, 0].astype(F32) + inbox[o, j, 3, i].astype(F32)
            both = both + inbox[o, j, 4, i].astype(F32)
            result[:, columns(2 * j + i)] = (both + inbox[o, j, 6, i].astype(F32)).astype(BF16)

    forward(0)
    second(DOWN)
    forward(1)
    fourth(GRAD)
    fourth(UP)
    third(DOWN)
    fifth(GATE)
    forward(2)
    fifth(GRAD)
    sixth(GRAD)
    fifth(UP)
    sixth(GATE)
    sixth(UP)
    forward(3)
    arrived(keep_buf.at[1], core_recv.at[3, 0], sibling)
    activate()
    from_sibling(DOWN, 0)
    from_sibling(DOWN, 1)
    out_part(0)
    sum_a(0, 0)
    backward(0)
    from_sibling(DOWN, 2)
    from_sibling(DOWN, 3)
    out_part(1)
    sum_a(0, 1)
    sum_b(0, 0)
    backward(1)
    fourth(DOWN)
    from_sibling(DOWN, 4)
    from_sibling(DOWN, 5)
    out_part(2)
    sum_a(0, 2)
    sum_b(0, 1)
    sum_c(0, 0)
    backward(2)
    fifth(DOWN)
    sum_b(0, 2)
    sum_c(0, 1)
    sum_d(0, 0)
    sixth(DOWN)
    from_sibling(DOWN, 6)
    from_sibling(DOWN, 7)
    backward(3)
    pull_back()
    grad_part(0)
    sum_a(1, 0)
    out_part(3)
    sum_a(0, 3)
    sum_c(0, 2)
    sum_d(0, 1)
    grad_part(1)
    sum_a(1, 1)
    sum_b(1, 0)
    sum_b(0, 3)
    grad_part(2)
    sum_a(1, 2)
    sum_b(1, 1)
    sum_c(1, 0)
    sum_d(0, 2)
    grad_part(3)
    sum_a(1, 3)
    sum_c(0, 3)
    sum_b(1, 2)
    sum_c(1, 1)
    sum_d(1, 0)
    sum_d(0, 3)
    sum_b(1, 3)
    sum_c(1, 2)
    sum_d(1, 1)
    sum_c(1, 3)
    sum_d(1, 2)
    sum_d(1, 3)
    for copy in sent:
        copy.wait_send()


def local(tokens, grad_out, gate_weight, up_weight, down_weight, keep_mask, task_ids):
    chunk, model = tokens.shape
    depth, hidden = gate_weight.shape
    width = KEPT * BLOCK
    s = lax.axis_index("seq")
    x, yh, core = s // 4, (s // 2) % 2, s % 2
    offset = jnp.array([0, 0, 1, 3, 1, 3, 2, 2], jnp.int32)
    other = jnp.array([0, 1, 0, 0, 1, 1, 0, 1], jnp.int32)
    owners = ((x + offset) % RING) * 4 + ((yh + other) % 2) * 2 + core
    tasks = jnp.take(task_ids.reshape(2 * SLOTS, chunk), owners, axis=0)
    padded = 2 * TASKS
    onehot = (tasks[:, :, None] == jnp.arange(padded, dtype=jnp.int32)).astype(BF16)
    onehot = onehot.reshape(SLOTS * chunk, padded)
    n_rows = SLOTS * chunk
    any_space, vmem = pl.BlockSpec(memory_space=pl.ANY), pl.BlockSpec(memory_space=pltpu.VMEM)
    dma = pltpu.SemaphoreType.DMA
    return pl.pallas_call(
        kernel,
        out_shape=[jax.ShapeDtypeStruct((chunk, model), BF16)] * 2,
        in_specs=[pl.BlockSpec(memory_space=pltpu.SMEM)] + [any_space] * 5 + [vmem],
        out_specs=[vmem, vmem],
        scratch_shapes=[
            pltpu.VMEM((2, SLOTS, chunk, model), BF16),
            pltpu.VMEM((3, 2, SLOTS, depth, width), BF16),
            pltpu.VMEM((2, depth, hidden), BF16),
            pltpu.VMEM((hidden, depth), BF16),
            pltpu.VMEM((2, padded, width), BF16),
            pltpu.VMEM((3, n_rows, 2 * width), F32),
            pltpu.VMEM((n_rows, 2 * width), BF16),
            pltpu.VMEM((n_rows, 2 * width), BF16),
            pltpu.VMEM((n_rows, 2 * width), BF16),
            pltpu.VMEM((2, SLOTS, SLOTS, chunk, width), BF16),
            pltpu.VMEM((2, PAIRS, 7, 2, chunk, width), BF16),
            dma((6,)),
            dma((5, 9)),
            dma((5, SLOTS + 2)),
            dma((4, SLOTS)),
            dma((4, SLOTS)),
            dma((2, PAIRS, 7)),
            dma((2, PAIRS, 7)),
        ],
        compiler_params=pltpu.CompilerParams(
            collective_id=0, has_side_effects=True, vmem_limit_bytes=64_000_000
        ),
        name="swiglu",
    )(keep_mask, tokens, grad_out, gate_weight, up_weight, down_weight, onehot)


def solution(mesh):
    placed = (
        P(("fsdp", "seq"), None),
        P(("fsdp", "seq"), None),
        P("fsdp", "seq"),
        P("fsdp", "seq"),
        P("seq", "fsdp"),
        P(None, "seq"),
        P("fsdp"),
    )
    return jax.shard_map(
        local,
        mesh=mesh,
        in_specs=placed,
        out_specs=(P(("fsdp", "seq"), None), P(("fsdp", "seq"), None)),
        check_vma=False,
    )
```

```python
import functools

import jax
import jax.numpy as jnp
from jax import lax
from jax.experimental import pallas as pl
from jax.experimental.pallas import tpu as pltpu
from jax.sharding import PartitionSpec as P

MESH = pl.DeviceIdType.MESH
F32, BF16 = jnp.float32, jnp.bfloat16
RING, PAIRS, SLOTS = 4, 4, 8
KEPT, BLOCK, TASKS = 4, 128, 8
TOK, GRAD, GATE, UP, DOWN = range(5)
BY_PAIR = (GATE,)
PAIR_FIRST = ((0, 3), (1, 1))


def dot(left, right):
    return jnp.dot(left, right, preferred_element_type=F32)


def dot_t(left, right):
    return lax.dot_general(left, right, (((1,), (1,)), ((), ())), preferred_element_type=F32)


def kernel(
    keep_ref, tok_ref, grad_ref, gate_ref, up_ref, down_ref, onehot_ref, out_ref, ig_ref,
    rows_buf, w_buf, cols_stage, rows_stage, keep_buf, acc, hid, gate_g, up_g, part, inbox,
    local_sem, send_sem, recv_sem, core_send, core_recv, rs_send, rs_recv,
):
    f, s = lax.axis_index("fsdp"), lax.axis_index("seq")
    z, yl = f % RING, f // RING
    x, yh, core = s // 4, (s // 2) % 2, s % 2
    x_up = {"seq": ((x + 1) % RING) * 4 + yh * 2 + core}
    x_down = {"seq": ((x + RING - 1) % RING) * 4 + yh * 2 + core}
    y_far = {"seq": x * 4 + (1 - yh) * 2 + core}
    sibling = {"seq": x * 4 + yh * 2 + 1 - core}
    z_up = {"fsdp": yl * RING + (z + 1) % RING}
    z_down = {"fsdp": yl * RING + (z + RING - 1) % RING}
    y_near = {"fsdp": (1 - yl) * RING + z}

    width = w_buf.shape[-1]
    chunk = tok_ref.shape[0]
    n_rows = SLOTS * chunk

    def owner(k):
        offset = (0, 0, 1, RING - 1, 1, RING - 1, 2, 2)[k]
        other = k in (1, 4, 5, 7)
        return ((1 - yl) if other else yl) * RING + (z + offset) % RING

    def columns(k):
        return pl.ds(pl.multiple_of(owner(k) * width, width), width)

    def slot(array, k):
        if array in (TOK, GRAD):
            return rows_buf.at[array, k]
        return w_buf.at[array - GATE, 0, k]

    def neighbours(array):
        return (x_up, x_down, y_far) if array in (TOK, GRAD) else (z_up, z_down, y_near)

    sent, seen_halves, lanes = [], set(), [0] * 5

    def send(src, dst, ssem, rsem, device):
        copy = pltpu.make_async_remote_copy(
            src_ref=src, dst_ref=dst, send_sem=ssem, recv_sem=rsem, device_id=device,
            device_id_type=MESH,
        )
        copy.start()
        sent.append(copy)

    def arrived(dst, rsem, device):
        pltpu.make_async_remote_copy(
            src_ref=dst, dst_ref=dst, send_sem=local_sem.at[0], recv_sem=rsem, device_id=device,
            device_id_type=MESH,
        ).wait_recv()

    def half_of(array, ref, h):
        if array in (TOK, GRAD):
            return ref.at[:, pl.ds(h * (ref.shape[1] // 2), ref.shape[1] // 2)]
        return ref.at[pl.ds(h * (ref.shape[0] // 2), ref.shape[0] // 2)]

    UPWARD, DOWNWARD, ACROSS = range(3)

    def move(array, k, h, hop, to, src=None):
        source = slot(array, k) if src is None else src
        lane = lanes[array]
        lanes[array] += 1
        send(
            half_of(array, source, h), half_of(array, slot(array, to), h), send_sem.at[array, lane],
            recv_sem.at[array, 2 * to + h], neighbours(array)[hop],
        )

    def to_sibling(array, k):
        w = array - GATE
        send(w_buf.at[w, 0, k], w_buf.at[w, 1, k], core_send.at[w, k], core_recv.at[w, k], sibling)

    def from_sibling(array, k):
        w = array - GATE
        arrived(w_buf.at[w, 1, k], core_recv.at[w, k], sibling)

    def need(array, k, h=None):
        for half in (0, 1) if h is None else (h,):
            if (array, k, half) in seen_halves:
                continue
            arrived(half_of(array, slot(array, k), half), recv_sem.at[array, 2 * k + half], sibling)
            seen_halves.add((array, k, half))
            if array >= GATE and (array, k, 1 - half) in seen_halves:
                to_sibling(array, k)

    def start(array, src=None):
        for h in (0, 1):
            move(array, 0, h, ACROSS, 1, src)
            move(array, 0, h, UPWARD, 3, src)
            move(array, 0, 1 - h, DOWNWARD, 2, src)
        if array >= GATE:
            to_sibling(array, 0)

    def second(array):
        need(array, 1, 0)
        move(array, 1, 0, UPWARD, 5)
        need(array, 1, 1)
        move(array, 1, 1, DOWNWARD, 4)
        move(array, 1, 1, UPWARD, 5)
        move(array, 1, 0, DOWNWARD, 4)

    def relay_own(array):
        need(array, 3, 0)
        move(array, 3, 0, UPWARD, 6)
        need(array, 2, 1)
        move(array, 2, 1, DOWNWARD, 6)

    def relay_other(array):
        if array in BY_PAIR:
            for h in (0, 1):
                need(array, 6, h)
                move(array, 6, h, ACROSS, 7)
        else:
            need(array, 5, 0)
            move(array, 5, 0, UPWARD, 7)
            need(array, 4, 1)
            move(array, 4, 1, DOWNWARD, 7)

    barrier = pltpu.get_barrier_semaphore()
    around = (x_up, x_down, y_far, sibling, z_up, z_down, y_near)
    for device in around:
        pl.semaphore_signal(barrier, inc=1, device_id=device, device_id_type=MESH)
    stage = (
        pltpu.make_async_copy(gate_ref, cols_stage.at[0], local_sem.at[1]),
        pltpu.make_async_copy(up_ref, cols_stage.at[1], local_sem.at[2]),
        pltpu.make_async_copy(down_ref, rows_stage, local_sem.at[3]),
        pltpu.make_async_copy(tok_ref, rows_buf.at[TOK, 0], local_sem.at[4]),
        pltpu.make_async_copy(grad_ref, rows_buf.at[GRAD, 0], local_sem.at[5]),
    )
    for copy in stage:
        copy.start()

    n_blocks = keep_ref.shape[1]
    spare = n_blocks - KEPT
    alive = []
    for b in range(n_blocks):
        seen = keep_ref[0, b]
        for t in range(1, TASKS):
            seen = jnp.maximum(seen, keep_ref[t, b])
        alive.append(seen)
    room = KEPT - sum(alive[1:], alive[0])
    taken, place, before = [], [], jnp.int32(0)
    for b in range(n_blocks):
        fill = (1 - alive[b]) * jnp.where(room > 0, 1, 0)
        room = room - fill
        taken.append(alive[b] + fill)
        place.append(before)
        before = before + taken[b]
    picks = [
        [(b, taken[b] * jnp.where(place[b] == j, 1, 0)) for b in range(j, j + spare + 1)]
        for j in range(KEPT)
    ]

    pl.semaphore_wait(barrier, len(around))
    start(TOK, tok_ref)

    def blend(terms, shape):
        blend_of = None
        for take, block in terms:
            term = block * jnp.full(shape, take.astype(F32)).astype(BF16)
            blend_of = term if blend_of is None else blend_of + term
        return blend_of

    def pack_columns(array):
        w = array - GATE
        stage[w].wait()
        step = 64

        @pl.loop(0, w_buf.shape[3] // step)
        def _(i):
            at = pl.ds(pl.multiple_of(i * step, step), step)
            for j in range(KEPT):
                terms = [(take, cols_stage[w, at, b * BLOCK : (b + 1) * BLOCK]) for b, take in picks[j]]
                w_buf[w, 0, 0, at, j * BLOCK : (j + 1) * BLOCK] = blend(terms, (step, BLOCK))

    pack_columns(GATE)
    start(GATE)
    pack_columns(UP)
    start(UP)
    start(GRAD, grad_ref)
    stage[2].wait()
    step = 32

    @pl.loop(0, BLOCK // step)
    def _(i):
        for j in range(KEPT):
            terms = [
                (take, rows_stage[pl.ds(pl.multiple_of(b * BLOCK + i * step, step), step), :])
                for b, take in picks[j]
            ]
            at = pl.ds(pl.multiple_of(j * BLOCK + i * step, step), step)
            w_buf[2, 0, 0, at, :] = blend(terms, (step, width))

    task_row = lax.broadcasted_iota(jnp.int32, (keep_buf.shape[1], BLOCK), 0)
    for j in range(KEPT):
        block = jnp.zeros((keep_buf.shape[1], BLOCK), F32)
        for t in range(TASKS):
            kept = sum(take * keep_ref[t, b] for b, take in picks[j])
            block = jnp.where(task_row == t, kept.astype(F32), block)
        keep_buf[0, :, j * BLOCK : (j + 1) * BLOCK] = block.astype(BF16)

    send(keep_buf.at[0], keep_buf.at[1], core_send.at[3, 0], core_recv.at[3, 0], sibling)
    stage[3].wait()
    stage[4].wait()

    def rows(array, k):
        return rows_buf[array, :, :, columns(k)].reshape(n_rows, width)

    def group(c):
        return pl.ds(pl.multiple_of(c * width, width), width)

    def forward(j):
        a, b = 2 * j, 2 * j + 1
        for array in (GATE, UP):
            for k in (a, b):
                if k:
                    need(array, k)
        for array in (GATE, UP):
            from_sibling(array, a)
            from_sibling(array, b)

        @pl.loop(0, 2)
        def _(c):
            for w in range(2):
                new = dot(rows(TOK, a), w_buf[w, c, a]) + dot(rows(TOK, b), w_buf[w, c, b])
                if j:
                    new = acc[w, :, group(c)] + new
                acc[w, :, group(c)] = new

    def backward(j):
        a, b = 2 * j, 2 * j + 1

        @pl.loop(0, 2)
        def _(c):
            new = dot_t(rows(GRAD, a), w_buf[2, c, a]) + dot_t(rows(GRAD, b), w_buf[2, c, b])
            if j:
                new = acc[2, :, group(c)] + new
            acc[2, :, group(c)] = new

    def activate():
        step = 32

        @pl.loop(0, n_rows // step)
        def _(i):
            at = pl.ds(pl.multiple_of(i * step, step), step)
            for c in range(2):
                cols = slice(c * width, (c + 1) * width)
                mask = dot(onehot_ref[at, :], keep_buf[c])
                gate_pre, up_pre = acc[0, at, cols], acc[1, at, cols]
                logistic = jax.nn.sigmoid(gate_pre)
                activated = gate_pre * logistic * mask
                hid[at, cols] = (activated * up_pre).astype(BF16)
                acc[0, at, cols] = mask * up_pre * logistic * (1.0 + gate_pre * (1.0 - logistic))
                acc[1, at, cols] = activated

    def pull_back():
        step = 32

        @pl.loop(0, n_rows // step)
        def _(i):
            at = pl.ds(pl.multiple_of(i * step, step), step)
            hidden_grad = acc[2, at, :]
            gate_g[at, :] = (hidden_grad * acc[0, at, :]).astype(BF16)
            up_g[at, :] = (hidden_grad * acc[1, at, :]).astype(BF16)

    def ready(j):
        for k in (2 * j, 2 * j + 1):
            if k:
                need(DOWN, k)
        for k in (2 * j, 2 * j + 1):
            from_sibling(DOWN, k)

    def out_part(j):
        @pl.loop(2 * j, 2 * j + 2)
        def _(k):
            new = dot(hid[:, :width], w_buf[2, 0, k]) + dot(hid[:, width:], w_buf[2, 1, k])
            part[0, k] = new.reshape(SLOTS, chunk, width).astype(BF16)

    def grad_part(j):
        @pl.loop(2 * j, 2 * j + 2)
        def _(k):
            new = dot_t(gate_g[:, :width], w_buf[0, 0, k]) + dot_t(gate_g[:, width:], w_buf[0, 1, k])
            new += dot_t(up_g[:, :width], w_buf[1, 0, k]) + dot_t(up_g[:, width:], w_buf[1, 1, k])
            part[1, k] = new.reshape(SLOTS, chunk, width).astype(BF16)

    def piece(o, j, at):
        return part.at[o, pl.ds(2 * j, 2), at]

    def post(o, j, at, m, device):
        send(piece(o, j, at), inbox.at[o, j, m], rs_send.at[o, j, m], rs_recv.at[o, j, m], device)

    def collect(o, j, m):
        arrived(inbox.at[o, j, m], rs_recv.at[o, j, m], sibling)

    def add(o, j, at, m, i):
        both = part[o, 2 * j + i, at].astype(F32) + inbox[o, j, m, i].astype(F32)
        part[o, 2 * j + i, at] = both.astype(BF16)

    def finish(o, j, terms):
        result = out_ref if o == 0 else ig_ref
        for i in range(2):
            both = part[o, 2 * j + i, 0].astype(F32)
            for m in terms:
                both = both + inbox[o, j, m, i].astype(F32)
            result[:, columns(2 * j + i)] = both.astype(BF16)

    def sum_a(o, j):
        if (o, j) in PAIR_FIRST:
            for m, at in ((3, 7), (1, 4), (2, 5), (0, 1)):
                post(o, j, at, m, y_far)
            return
        post(o, j, 6, 0, x_up)
        post(o, j, 7, 1, x_down)
        post(o, j, 4, 2, x_up)
        post(o, j, 3, 3, x_down)

    def sum_b(o, j):
        if (o, j) in PAIR_FIRST:
            collect(o, j, 3)
            for i, device in ((0, x_up), (1, x_down)):
                add(o, j, 6, 3, i)
                send(
                    part.at[o, 2 * j + i, 6], inbox.at[o, j, 4, i], rs_send.at[o, j, 4 + 3 * i],
                    rs_recv.at[o, j, 4 + 3 * i], device,
                )
            for m, at in ((1, 2), (2, 3)):
                collect(o, j, m)
                for i in range(2):
                    add(o, j, at, m, i)
            return
        for m, at, device in ((0, 2, x_up), (1, 5, x_down)):
            collect(o, j, m)
            for i in range(2):
                add(o, j, at, m, i)
            post(o, j, at, 4 + m, device)

    def sum_c(o, j):
        if (o, j) in PAIR_FIRST:
            for i, at, device in ((0, 2, x_up), (1, 3, x_down)):
                arrived(inbox.at[o, j, 4, i], rs_recv.at[o, j, 4 + 3 * i], sibling)
                add(o, j, at, 4, i)
                post(o, j, at, 5 + i, device)
            return
        for m in (2, 3, 4, 5):
            collect(o, j, m)
        for i in range(2):
            both = part[o, 2 * j + i, 1].astype(F32) + inbox[o, j, 2, i].astype(F32)
            part[o, 2 * j + i, 1] = (both + inbox[o, j, 5, i].astype(F32)).astype(BF16)
        post(o, j, 1, 6, y_far)

    def sum_d(o, j):
        if (o, j) in PAIR_FIRST:
            for m in (0, 5, 6):
                collect(o, j, m)
            finish(o, j, (0, 5, 6))
            return
        collect(o, j, 6)
        finish(o, j, (3, 4, 6))

    relay_own(GATE)
    relay_own(TOK)
    second(TOK)
    second(GATE)
    relay_own(UP)
    relay_other(TOK)
    relay_other(GATE)
    second(UP)
    relay_own(GRAD)
    second(GRAD)
    for k in range(1, SLOTS):
        need(TOK, k)
    for k in (2, 3):
        need(GATE, k)
        need(UP, k)
    forward(0)
    forward(1)
    relay_other(UP)
    start(DOWN)
    relay_other(GRAD)
    forward(2)
    forward(3)
    arrived(keep_buf.at[1], core_recv.at[3, 0], sibling)
    activate()
    second(DOWN)
    relay_own(DOWN)
    for k in range(1, SLOTS):
        need(GRAD, k)
    ready(0)
    out_part(0)
    sum_a(0, 0)
    backward(0)
    ready(1)
    out_part(1)
    sum_a(0, 1)
    sum_b(0, 0)
    backward(1)
    relay_other(DOWN)
    sum_b(0, 1)
    sum_c(0, 0)
    sum_c(0, 1)
    ready(2)
    out_part(2)
    sum_a(0, 2)
    backward(2)
    sum_d(0, 0)
    ready(3)
    out_part(3)
    sum_a(0, 3)
    backward(3)
    sum_b(0, 2)
    sum_d(0, 1)
    pull_back()
    grad_part(0)
    sum_a(1, 0)
    sum_b(0, 3)
    sum_c(0, 2)
    grad_part(1)
    sum_a(1, 1)
    sum_b(1, 0)
    sum_c(0, 3)
    grad_part(2)
    sum_a(1, 2)
    sum_b(1, 1)
    sum_c(1, 0)
    sum_d(0, 2)
    grad_part(3)
    sum_a(1, 3)
    sum_d(0, 3)
    sum_b(1, 2)
    sum_c(1, 1)
    sum_d(1, 0)
    sum_b(1, 3)
    sum_c(1, 2)
    sum_d(1, 1)
    sum_c(1, 3)
    sum_d(1, 2)
    sum_d(1, 3)
    for copy in sent:
        copy.wait_send()


def local(tokens, grad_out, gate_weight, up_weight, down_weight, keep_mask, task_ids):
    chunk, model = tokens.shape
    depth, hidden = gate_weight.shape
    width = KEPT * BLOCK
    s = lax.axis_index("seq")
    x, yh, core = s // 4, (s // 2) % 2, s % 2
    offset = jnp.array([0, 0, 1, 3, 1, 3, 2, 2], jnp.int32)
    other = jnp.array([0, 1, 0, 0, 1, 1, 0, 1], jnp.int32)
    owners = ((x + offset) % RING) * 4 + ((yh + other) % 2) * 2 + core
    tasks = jnp.take(task_ids.reshape(2 * SLOTS, chunk), owners, axis=0)
    padded = 2 * TASKS
    onehot = (tasks[:, :, None] == jnp.arange(padded, dtype=jnp.int32)).astype(BF16)
    onehot = onehot.reshape(SLOTS * chunk, padded)
    n_rows = SLOTS * chunk
    any_space, vmem = pl.BlockSpec(memory_space=pl.ANY), pl.BlockSpec(memory_space=pltpu.VMEM)
    dma = pltpu.SemaphoreType.DMA
    return pl.pallas_call(
        kernel,
        out_shape=[jax.ShapeDtypeStruct((chunk, model), BF16)] * 2,
        in_specs=[pl.BlockSpec(memory_space=pltpu.SMEM)] + [any_space] * 5 + [vmem],
        out_specs=[vmem, vmem],
        scratch_shapes=[
            pltpu.VMEM((2, SLOTS, chunk, model), BF16),
            pltpu.VMEM((3, 2, SLOTS, depth, width), BF16),
            pltpu.VMEM((2, depth, hidden), BF16),
            pltpu.VMEM((hidden, depth), BF16),
            pltpu.VMEM((2, padded, width), BF16),
            pltpu.VMEM((3, n_rows, 2 * width), F32),
            pltpu.VMEM((n_rows, 2 * width), BF16),
            pltpu.VMEM((n_rows, 2 * width), BF16),
            pltpu.VMEM((n_rows, 2 * width), BF16),
            pltpu.VMEM((2, SLOTS, SLOTS, chunk, width), BF16),
            pltpu.VMEM((2, PAIRS, 7, 2, chunk, width), BF16),
            dma((6,)),
            dma((5, 14)),
            dma((5, 2 * SLOTS)),
            dma((4, SLOTS)),
            dma((4, SLOTS)),
            dma((2, PAIRS, 8)),
            dma((2, PAIRS, 8)),
        ],
        compiler_params=pltpu.CompilerParams(
            collective_id=0, has_side_effects=True, vmem_limit_bytes=64_000_000
        ),
        name="swiglu",
    )(keep_mask, tokens, grad_out, gate_weight, up_weight, down_weight, onehot)


def solution(mesh):
    placed = (
        P(("fsdp", "seq"), None),
        P(("fsdp", "seq"), None),
        P("fsdp", "seq"),
        P("fsdp", "seq"),
        P("seq", "fsdp"),
        P(None, "seq"),
        P("fsdp"),
    )
    return jax.shard_map(
        local,
        mesh=mesh,
        in_specs=placed,
        out_specs=(P(("fsdp", "seq"), None), P(("fsdp", "seq"), None)),
        check_vma=False,
    )
```
